32 devices in a mesh: fsdp: 4 (over x, core), ctx: 8 (over z, y).
Axes of the slice: x: 2, y: 2, z: 4, core: 2. Of those that a mesh axis runs over, the one named last changes fastest.
Arguments:
- tokens: bfloat16 [4, 1024, 2048], P('fsdp', 'ctx'), may hold values from -6 to 6
- block_order: int32 [16], replicated, may hold values from 0 to 15, each once
- ln1_gain: float32 [2048], replicated, may hold values from 0.1 to 1.9
- ln1_bias: float32 [2048], replicated, may hold values from -1.75 to 1.75
- ln2_gain: float32 [2048], replicated, may hold values from 0.1 to 1.9
- ln2_bias: float32 [2048], replicated, may hold values from -1.75 to 1.75
- w_qkv: bfloat16 [2048, 6144], P('fsdp'), may hold values from -0.125 to 0.125
- b_qkv: float32 [6144], replicated, may hold values from -0.625 to 0.625
- w_dense: bfloat16 [2048, 2048], P('fsdp'), may hold values from -1 to 1
- b_dense: float32 [2048], replicated, may hold values from -1.75 to 1.75
- w_fc1: bfloat16 [2048, 8192], P('fsdp'), may hold values from -0.125 to 0.125
- b_fc1: float32 [8192], replicated, may hold values from -1.75 to 1.75
- w_fc2: bfloat16 [8192, 2048], P('fsdp'), may hold values from -0.0625 to 0.0625
- b_fc2: float32 [2048], replicated, may hold values from -1.75 to 1.75
- cotangent: bfloat16 [4, 1024, 2048], P('fsdp', 'ctx'), may hold values from -6 to 6
Outputs:
- out: bfloat16 [4, 1024, 2048], P('fsdp', 'ctx')
- d_tokens: bfloat16 [4, 1024, 2048], P('fsdp', 'ctx')
- d_ln1_gain: float32 [2048], P(('fsdp', 'ctx'))
- d_ln1_bias: float32 [2048], P(('fsdp', 'ctx'))
- d_ln2_gain: float32 [2048], P(('fsdp', 'ctx'))
- d_ln2_bias: float32 [2048], P(('fsdp', 'ctx'))
- d_w_qkv: float32 [2048, 6144], P(('fsdp', 'ctx'))
- d_b_qkv: float32 [6144], P(('fsdp', 'ctx'))
- d_w_dense: float32 [2048, 2048], P(('fsdp', 'ctx'))
- d_b_dense: float32 [2048], P(('fsdp', 'ctx'))
- d_w_fc1: float32 [2048, 8192], P(('fsdp', 'ctx'))
- d_b_fc1: float32 [8192], P(('fsdp', 'ctx'))
- d_w_fc2: float32 [8192, 2048], P(('fsdp', 'ctx'))
- d_b_fc2: float32 [2048], P(('fsdp', 'ctx'))
The draws below stay inside these ranges and needn't reach their ends.
Inputs may be any that keep to these rules, and one draw needn't show every extreme that they name: `block_order`: a permutation: entry j is the block of 64 positions stored in place j of every sequence.
All inputs are finite; a program needn't handle non-finite values.
Results may differ from the reference program's by a relative error of at most 0.035.
Values may be sent and summed in bfloat16 or wider, within the bound.
No kernel may reach another device: no remote copies, remote signals or barrier semaphores. Data moves between devices by JAX's collectives and lax.ppermute only.
A program may use at most 704 MiB of HBM per device.

```python
import math
import jax
import jax.numpy as jnp
from jax import lax

D = 2048
FF = 8192
HEADS = 8
HEAD_DIM = 256
ROTARY = 64
TOK_SEQ = 128
BLOCKS = 16
LEN = 1024
SEQS_ALL = 4


def spiked(drawn, stream_key, source, target, shards_of, factor):
    def block_of(dim):
        return (jnp.arange(drawn.shape[dim]) // (drawn.shape[dim] // shards_of)).reshape((-1,) + (1,) * (drawn.ndim - 1 - dim))

    first = jax.random.permutation(stream_key, shards_of)[block_of(target)]
    far = (block_of(target) + shards_of // 2) % shards_of
    return jnp.where((block_of(source) == first) | (block_of(source) == far), factor * drawn, drawn)


def shard_levels(stream_key, extent, cuts, least, top_value):
    def one(position, parts):
        draws = jax.random.uniform(jax.random.fold_in(jax.random.fold_in(stream_key, 6), position), (parts,), jnp.float32, least / len(cuts), top_value / len(cuts))
        return jnp.repeat(jnp.exp(draws), extent[position] // parts).reshape((-1,) + (1,) * (len(extent) - position - 1))

    factor_of = one(*cuts[0])
    for cut in cuts[1:]:
        factor_of = factor_of * one(*cut)
    return factor_of


def bell_draw(rng, dims, deviation, reach, cuts=(), kind=jnp.bfloat16):
    drawn = jax.random.normal(rng, dims, jnp.float32) * deviation
    if len(cuts) > 0:
        drawn = shard_levels(rng, dims, cuts, -0.22, 0.18) * drawn
    return jnp.clip(drawn, min=-reach, max=reach).astype(kind)


def heavy_noise(stream_key, dims, scale, bound, shards, heavy, kind=jnp.bfloat16):
    entries = scale * jax.random.normal(stream_key, dims, jnp.float32)
    if shards:
        entries = entries * shard_levels(stream_key, dims, shards, -0.22, 0.18)
    return jnp.clip(spiked(entries, jax.random.fold_in(stream_key, 3), *heavy), -bound, bound).astype(kind)


def setup_inputs(seed: int = 0) -> dict:
    streams_of = jax.random.split(jax.random.key(seed), 16)
    return {
        "tokens": bell_draw(streams_of[0], (SEQS_ALL, LEN, D), 1.0, 6.0, ((0, 4), (1, 8))),
        "block_order": jax.random.permutation(streams_of[1], BLOCKS).astype(jnp.int32),
        "ln1_gain": jnp.clip(1.0 + 0.18 * jax.random.normal(streams_of[2], (D,), jnp.float32), 0.1, 1.9),
        "ln1_bias": bell_draw(streams_of[3], (D,), 0.3, 1.75, (), jnp.float32),
        "ln2_gain": jnp.clip(1.0 + 0.18 * jax.random.normal(streams_of[4], (D,), jnp.float32), 0.1, 1.9),
        "ln2_bias": bell_draw(streams_of[5], (D,), 0.3, 1.75, (), jnp.float32),
        "w_qkv": bell_draw(streams_of[6], (D, 3 * D), D ** -0.5, 0.125, ((0, 4),)),
        "b_qkv": bell_draw(streams_of[7], (3 * D,), 0.1, 0.625, (), jnp.float32),
        "w_dense": bell_draw(streams_of[8], (D, D), (D // 64) ** -0.5, 1.0, ((0, 4),)),
        "b_dense": bell_draw(streams_of[9], (D,), 0.3, 1.75, (), jnp.float32),
        "w_fc1": bell_draw(streams_of[10], (D, FF), D ** -0.5, 0.125, ((0, 4),)),
        "b_fc1": bell_draw(streams_of[11], (FF,), 0.3, 1.75, (), jnp.float32),
        "w_fc2": bell_draw(streams_of[12], (FF, D), FF ** -0.5, 0.0625, ((0, 4),)),
        "b_fc2": bell_draw(streams_of[13], (D,), 0.3, 1.75, (), jnp.float32),
        "cotangent": heavy_noise(streams_of[14], (SEQS_ALL, LEN, D), 1.0, 6.0, ((0, 4), (1, 8)), (1, 2, 8, 2.0)),
    }


epsilon = 1e-05
big_negative = -1e+30

@jax.custom_vjp
def low(v):
    return lax.optimization_barrier(v.astype(jnp.bfloat16)).astype(jnp.float32)

@jax.custom_vjp
def low_back(v):
    return v

def low_keep(v):
    return (low(v), None)

def low_pass(kept, grad):
    return (grad,)

def back_keep(v):
    return (v, None)

def back_low(kept, grad):
    return (low(grad),)
low.defvjp(low_keep, low_pass)
low_back.defvjp(back_keep, back_low)

def layer_norm(values, gain, shift):
    center = values - lax.optimization_barrier(jnp.mean(values, axis=-1, keepdims=True))
    spread = lax.optimization_barrier(jnp.mean(center * center, axis=-1, keepdims=True))
    return center * lax.rsqrt(spread + epsilon) * gain + shift

def angles_of(positions):
    inverse_rate = 10000.0 ** (-jnp.arange(0, ROTARY, 2, dtype=jnp.float32) / ROTARY)
    phase = positions.astype(jnp.float32)[:, None] * inverse_rate[None, :]
    phase = jnp.concatenate([phase, phase], axis=-1)
    return (jnp.cos(phase), jnp.sin(phase))

def rotate(values, cosine, sine):
    head_part = values[..., :ROTARY]
    middle = ROTARY // 2
    turned = jnp.concatenate([-head_part[..., middle:], head_part[..., :middle]], axis=-1)
    mixed = head_part * cosine[:, None, :] + turned * sine[:, None, :]
    return jnp.concatenate([mixed, values[..., ROTARY:]], axis=-1)

def exact_gelu(values):
    return jax.nn.gelu(values, approximate=False)

def matmul(left, right):
    return jnp.dot(left, right, preferred_element_type=jnp.float32, precision=lax.Precision.HIGHEST)

def attend(query, key, value, positions):
    length = query.shape[0]
    block = math.gcd(length, 512)
    scale = HEAD_DIM ** (-0.5)

    def one_block(pair):
        query_block, block_pos = pair
        scores = jnp.einsum('qhd,khd->qhk', query_block, key, preferred_element_type=jnp.float32, precision=lax.Precision.HIGHEST) * scale
        scores = low_back(scores)
        visible = positions[None, :] <= block_pos[:, None]
        scores = jnp.where(visible[:, None, :], scores, big_negative)
        probs = low(jax.nn.softmax(scores, axis=-1))
        return jnp.einsum('qhk,khd->qhd', probs, value, preferred_element_type=jnp.float32, precision=lax.Precision.HIGHEST)
    blocks_out = lax.map(jax.checkpoint(one_block), (query.reshape(length // block, block, HEADS, HEAD_DIM), positions.reshape(length // block, block)))
    return blocks_out.reshape(length, HEADS, HEAD_DIM)

def layer(inputs, params, positions):
    ln1_gain, ln1_bias, ln2_gain, ln2_bias, w_qkv, b_qkv, w_dense, b_dense, w_fc1, b_fc1, w_fc2, b_fc2 = params
    length = inputs.shape[0]
    cosine, sine = angles_of(positions)
    normed_one = low(layer_norm(inputs, ln1_gain, ln1_bias))
    mixed = low_back(matmul(normed_one, w_qkv) + b_qkv)
    query, key, value = jnp.split(mixed, 3, axis=-1)
    shape3 = (length, HEADS, HEAD_DIM)
    query = low(rotate(query.reshape(shape3), cosine, sine))
    key = low(rotate(key.reshape(shape3), cosine, sine))
    value = low(value.reshape(shape3))
    attention = low_back(low(attend(query, key, value, positions).reshape(length, D)))
    branch_attention = matmul(attention, w_dense) + b_dense
    normed_two = low(layer_norm(inputs, ln2_gain, ln2_bias))
    hidden = low_back(matmul(normed_two, w_fc1) + b_fc1)
    activated = low(exact_gelu(hidden))
    branch_mlp = matmul(activated, w_fc2) + b_fc2
    return inputs + branch_attention + branch_mlp

def reference(tokens, block_order, ln1_gain, ln1_bias, ln2_gain, ln2_bias, w_qkv, b_qkv, w_dense, b_dense, w_fc1, b_fc1, w_fc2, b_fc2, cotangent):
    block_half = TOK_SEQ // 2
    row_ids = jnp.arange(LEN, dtype=jnp.int32)
    positions = block_order[row_ids // block_half].astype(jnp.int32) * block_half + row_ids % block_half
    params = (ln1_gain.astype(jnp.float32), ln1_bias.astype(jnp.float32), ln2_gain.astype(jnp.float32), ln2_bias.astype(jnp.float32), w_qkv.astype(jnp.float32), b_qkv.astype(jnp.float32), w_dense.astype(jnp.float32), b_dense.astype(jnp.float32), w_fc1.astype(jnp.float32), b_fc1.astype(jnp.float32), w_fc2.astype(jnp.float32), b_fc2.astype(jnp.float32))

    def forward(seq_input, param_set):
        return layer(seq_input, param_set, positions)

    def one_sequence(totals, pair):
        seq_input, seq_grad = pair
        outputs, pullback = jax.vjp(forward, seq_input.astype(jnp.float32), params)
        grad_input, grad_params = pullback(seq_grad.astype(jnp.float32))
        totals = jax.tree.map(jnp.add, totals, grad_params)
        return (totals, (outputs.astype(jnp.bfloat16), grad_input.astype(jnp.bfloat16)))
    zeros = jax.tree.map(jnp.zeros_like, params)
    totals, (outputs, grad_tokens) = lax.scan(one_sequence, zeros, (tokens, cotangent))
    return (outputs, grad_tokens, totals[0], totals[1], totals[2], totals[3], totals[4], totals[5], totals[6], totals[7], totals[8], totals[9], totals[10], totals[11])
```

```python
import jax
import jax.numpy as jnp
from jax import lax
from jax.sharding import PartitionSpec as P

HEADS = 8
HEAD_DIM = 256
ROTARY = 64

epsilon = 1e-05
big_negative = -1e30
BF = jnp.bfloat16
F32 = jnp.float32


def angles_of(positions):
    inverse_rate = 10000.0 ** (-jnp.arange(0, ROTARY, 2, dtype=F32) / ROTARY)
    phase = positions.astype(F32)[:, None] * inverse_rate[None, :]
    phase = jnp.concatenate([phase, phase], axis=-1)
    return (jnp.cos(phase), jnp.sin(phase))


def rotate(values, cosine, sine):
    head_part = values[..., :ROTARY]
    middle = ROTARY // 2
    turned = jnp.concatenate([-head_part[..., middle:], head_part[..., :middle]], axis=-1)
    mixed = head_part * cosine + turned * sine
    return jnp.concatenate([mixed, values[..., ROTARY:]], axis=-1)


def rotate_back(values, cosine, sine):
    head_part = values[..., :ROTARY]
    middle = ROTARY // 2
    scaled = head_part * sine
    turned = jnp.concatenate([scaled[..., middle:], -scaled[..., :middle]], axis=-1)
    mixed = head_part * cosine + turned
    return jnp.concatenate([mixed, values[..., ROTARY:]], axis=-1)


def exact_gelu(values):
    return jax.nn.gelu(values, approximate=False)


def positions_of(block_order, slices, local_len):
    block = local_len // 2
    rows = (slices[:, None] * local_len + jnp.arange(local_len, dtype=jnp.int32)[None, :]).reshape(-1)
    places = rows // block
    table = places[:, None] == jnp.arange(block_order.shape[0], dtype=jnp.int32)[None, :]
    chosen = jnp.sum(jnp.where(table, block_order[None, :], 0), axis=1)
    return chosen * block + rows % block


def dot(left, right, dims):
    return lax.dot_general(left, right, (dims, ((), ())), preferred_element_type=F32)


def pick(array, index, axis=0):
    return lax.dynamic_index_in_dim(array, index, axis, keepdims=False)


def make_shards(F, C):
    R = C // 2
    T = 2 * F
    bits = R.bit_length() - 1
    assert R == 1 << bits and F & (F - 1) == 0

    def swap_f(array, mask):
        return lax.ppermute(array, "fsdp", [(i, i ^ mask) for i in range(F)])

    def swap_c(array, mask):
        return lax.ppermute(array, "ctx", [(i, i ^ mask) for i in range(C)])

    def swap_fc(array, fmask, cmask):
        if cmask == 0:
            return swap_f(array, fmask)
        if fmask == 0:
            return swap_c(array, cmask)
        pairs = [
            (i * C + j, (i ^ fmask) * C + (j ^ cmask)) for i in range(F) for j in range(C)
        ]
        return lax.ppermute(array, ("fsdp", "ctx"), pairs)

    fbits = F.bit_length() - 1
    order = []
    for e in range(T):
        half = e & 1
        rest = e >> 1
        mask = 0
        for k in range(fbits):
            if (rest >> (fbits - 1 - k)) & 1:
                mask |= 1 << k
        order.append((mask, half))

    def gather_blocks(own):
        blocks = {(0, 0): own, (0, 1): swap_c(own, R)}
        for k in reversed(range(fbits)):
            for key in list(blocks):
                blocks[(key[0] | (1 << k), key[1])] = swap_f(blocks[key], 1 << k)
        return [blocks[key] for key in order]

    def scatter_blocks(array):
        current = array
        total = None
        for k in range(fbits):
            half = current.shape[0] // 2
            got = swap_f(current[half:], 1 << k)
            total = current[:half].astype(F32) + got.astype(F32)
            current = total.astype(BF)
        got = swap_c(current[1:], R)
        return total[0] + got[0].astype(F32)

    def columns_of_rows(weight, t, fi, half):
        rows, cols = weight.shape[0], weight.shape[2]
        out = jnp.zeros((F * rows, cols), weight.dtype)
        for e in range(F):
            block = pick(weight, ((fi ^ e) * 2 + half), 1)
            if e:
                block = swap_f(block, e)
            out = lax.dynamic_update_slice(out, block, ((fi ^ e) * rows, 0))
        return out

    def reduce_rest(array, ri, first_low):
        lead = array.shape[0]
        tail = array.shape[2:]
        order_bits = list(range(bits)) if first_low else list(reversed(range(bits)))
        current = array.reshape((lead,) + (2,) * bits + tail)
        live = list(reversed(range(bits)))
        total = None
        for k in order_bits:
            axis = 1 + live.index(k)
            mine = (ri >> k) & 1
            sent = pick(current, 1 - mine, axis).astype(BF)
            kept = pick(current, mine, axis)
            got = swap_c(sent, 1 << k)
            current = kept.astype(F32) + got.astype(F32)
            live.remove(k)
        return current

    def columns_back(array, t, fi, half):
        low = array.astype(BF)
        blocks = []
        for e in range(T):
            sent = pick(low, t ^ e)
            blocks.append(sent if e == 0 else swap_fc(sent, e >> 1, R * (e & 1)))
        stacked = jnp.stack(blocks)
        return jnp.stack([pick(stacked, t ^ j) for j in range(T)], axis=0).astype(F32)

    def spread_attention(qkv, grad_heads, block_order, fi, half, ri, local_len):
        scale = HEAD_DIM ** (-0.5)
        count = R * qkv.shape[1]

        def exchange_in(array):
            parts = []
            for s in range(R):
                sent = pick(array, ri ^ s)
                parts.append(sent if s == 0 else swap_c(sent, s))
            return jnp.concatenate(parts, axis=0)

        def exchange_out(array):
            parts = array.reshape((R, count // R) + array.shape[1:])
            got = [parts[s] if s == 0 else swap_c(parts[s], s) for s in range(R)]
            stacked = jnp.stack(got)
            return jnp.stack([pick(stacked, ri ^ j) for j in range(R)])

        whole = exchange_in(qkv)
        grads = exchange_in(grad_heads)
        slices = jnp.stack(
            [(half ^ j) * R + (ri ^ s) for s in range(R) for j in range(2)]
        ).astype(jnp.int32)
        pos = positions_of(block_order, slices, local_len)
        query, key, value = whole[:, 0], whole[:, 1], whole[:, 2]
        visible = pos[None, :] <= pos[:, None]
        scores = jnp.where(visible, dot(query, key, ((1,), (1,))) * scale, big_negative)
        top = jnp.max(scores, axis=-1, keepdims=True)
        weights = jnp.where(visible, jnp.exp(scores - top), 0.0)
        probs = weights / jnp.sum(weights, axis=-1, keepdims=True)
        probs_low = probs.astype(BF)
        attention = dot(probs_low, value, ((1,), (0,)))
        attention_low = exchange_out(attention.astype(BF))
        delta = jnp.sum(grads.astype(F32) * attention, axis=-1, keepdims=True)
        grad_probs = dot(grads, value, ((1,), (1,)))
        grad_scores = (probs * (grad_probs - delta)).astype(BF)
        grad_query = dot(grad_scores, key, ((1,), (0,))) * scale
        grad_key = dot(grad_scores, query, ((0,), (0,))) * scale
        grad_value = dot(probs_low, grads, ((0,), (0,)))
        cosine, sine = angles_of(pos)
        grad_mixed = jnp.stack(
            [rotate_back(grad_query, cosine, sine), rotate_back(grad_key, cosine, sine), grad_value],
            axis=1,
        ).astype(BF)
        return attention_low, exchange_out(grad_mixed)

    def gathered_attention(qkv, grad_heads, block_order, fi, half, ri, local_len):
        scale = HEAD_DIM ** (-0.5)
        query, pair = qkv[:, :, 0], qkv[:, :, 1:]
        pairs = pair[None]
        for k in range(bits):
            pairs = jnp.concatenate([pairs, swap_c(pairs, 1 << k)], axis=0)
        my_slices = jnp.stack([(half ^ j) * R + ri for j in range(2)]).astype(jnp.int32)
        all_slices = jnp.stack(
            [(half ^ j) * R + (ri ^ s) for s in range(R) for j in range(2)]
        ).astype(jnp.int32)
        pos = positions_of(block_order, my_slices, local_len)
        key_pos = positions_of(block_order, all_slices, local_len)
        key = jnp.moveaxis(pairs[:, :, :, 0], 0, 1).reshape(qkv.shape[0], -1, HEAD_DIM)
        value = jnp.moveaxis(pairs[:, :, :, 1], 0, 1).reshape(qkv.shape[0], -1, HEAD_DIM)
        visible = (key_pos[None, :] <= pos[:, None])[None]

        def product(spec, a, b):
            return jnp.einsum(spec, a, b, preferred_element_type=F32)

        scores = jnp.where(visible, product("sqd,skd->sqk", query, key) * scale, big_negative)
        top = jnp.max(scores, axis=-1, keepdims=True)
        weights = jnp.where(visible, jnp.exp(scores - top), 0.0)
        probs = weights / jnp.sum(weights, axis=-1, keepdims=True)
        probs_low = probs.astype(BF)
        attention = product("sqk,skd->sqd", probs_low, value)
        delta = jnp.sum(grad_heads.astype(F32) * attention, axis=-1, keepdims=True)
        grad_probs = product("sqd,skd->sqk", grad_heads, value)
        grad_scores = (probs * (grad_probs - delta)).astype(BF)
        grad_query = product("sqk,skd->sqd", grad_scores, key) * scale
        grad_key = product("sqk,sqd->skd", grad_scores, query) * scale
        grad_value = product("sqk,sqd->skd", probs_low, grad_heads)
        both = jnp.stack([grad_key, grad_value], axis=2)
        both = both.reshape((qkv.shape[0], R, qkv.shape[1], 2, HEAD_DIM))
        both = jnp.moveaxis(both, 1, 0)
        for k in reversed(range(bits)):
            rest = both.shape[0] // 2
            both = both[:rest] + swap_c(both[rest:], 1 << k)
        cosine, sine = angles_of(pos)
        grad_mixed = jnp.stack(
            [
                rotate_back(grad_query, cosine, sine),
                rotate_back(both[0, :, :, 0], cosine, sine),
                both[0, :, :, 1],
            ],
            axis=2,
        ).astype(BF)
        return attention.astype(BF), grad_mixed

    def shards(
        tokens,
        block_order,
        ln1_gain,
        ln1_bias,
        ln2_gain,
        ln2_bias,
        w_qkv,
        b_qkv,
        w_dense,
        b_dense,
        w_fc1,
        b_fc1,
        w_fc2,
        b_fc2,
        cotangent,
    ):
        seqs, local_len, width = tokens.shape
        hidden_width = w_fc1.shape[1]
        rows = seqs * local_len
        count = T * rows
        head = HEADS // T * HEAD_DIM
        assert head == HEAD_DIM
        cols = hidden_width // T
        fi = lax.axis_index("fsdp")
        ci = lax.axis_index("ctx")
        half = ci // R
        ri = ci % R
        t = fi * 2 + half

        own = tokens.reshape(rows, width)
        own_grad = cotangent.reshape(rows, width)
        token_blocks = gather_blocks(own)
        fc1 = columns_of_rows(w_fc1.reshape(-1, T, cols), t, fi, half)
        grad_blocks = gather_blocks(own_grad)
        qkv_rows = jnp.moveaxis(w_qkv.reshape(-1, 3, T, head), 1, 2).reshape(-1, T, 3 * head)
        wq = columns_of_rows(qkv_rows, t, fi, half)
        inputs = jnp.concatenate(token_blocks, axis=0).astype(F32)
        grads = jnp.concatenate(grad_blocks, axis=0)

        def norm_parts(values):
            center = values - jnp.mean(values, axis=-1, keepdims=True)
            spread = jnp.mean(center * center, axis=-1, keepdims=True)
            factor = lax.rsqrt(spread + epsilon)
            return center * factor, factor

        xhat, _ = norm_parts(inputs)
        normed_one = (xhat * ln1_gain + ln1_bias).astype(BF)
        normed_two = (xhat * ln2_gain + ln2_bias).astype(BF)

        fc2 = pick(w_fc2.reshape(2, cols, width), half)
        hidden = dot(normed_two, fc1, ((1,), (0,))) + pick(b_fc1.reshape(T, cols), t)
        activated, gelu_back = jax.vjp(exact_gelu, hidden)
        activated_low = activated.astype(BF)
        (grad_hidden,) = gelu_back(dot(grads, fc2, ((1,), (1,))))
        grad_hidden_low = grad_hidden.astype(BF)
        fc2_term = dot(activated_low, grads, ((0,), (0,))).astype(BF)
        fc1_term = dot(normed_two, grad_hidden_low, ((0,), (0,))).astype(BF)

        dense = pick(w_dense.reshape(2, head, width), half)
        bias = pick(b_qkv.reshape(3, T, head), t, 1)
        mixed = dot(normed_one, wq, ((1,), (0,))).reshape(count, 3, head) + bias[None]
        my_slices = jnp.stack([(half ^ j) * R + ri for j in range(2)]).astype(jnp.int32)
        cosine, sine = angles_of(positions_of(block_order, my_slices, local_len))
        mixed = mixed.reshape(F, 2, seqs, local_len, 3, head)
        mixed = jnp.moveaxis(mixed, 2, 1).reshape(F * seqs, 2 * local_len, 3, head)
        qkv = jnp.stack(
            [
                rotate(mixed[:, :, 0], cosine, sine),
                rotate(mixed[:, :, 1], cosine, sine),
                mixed[:, :, 2],
            ],
            axis=2,
        ).astype(BF)
        grad_heads = dot(grads, dense, ((1,), (1,))).astype(BF)
        grad_heads = jnp.moveaxis(grad_heads.reshape(F, 2, seqs, local_len, head), 2, 1)
        grad_heads = grad_heads.reshape(F * seqs, 2 * local_len, head)
        attend = spread_attention if F * seqs == R else gathered_attention
        attention_low, grad_mixed = attend(qkv, grad_heads, block_order, fi, half, ri, local_len)

        def tokens_order(array):
            array = array.reshape((F, seqs, 2, local_len) + array.shape[2:])
            return jnp.moveaxis(array, 1, 2).reshape((count,) + array.shape[4:])

        attention_low = tokens_order(attention_low)
        grad_mixed = tokens_order(grad_mixed).reshape(count, 3 * head)

        partial = dot(activated_low, fc2, ((1,), (0,))) + dot(attention_low, dense, ((1,), (0,)))
        summed = scatter_blocks(partial.astype(BF).reshape(T, rows, width))
        own_f32 = own.astype(F32)
        output = (own_f32 + (summed + b_dense + b_fc2)).astype(BF)

        back_two = dot(grad_hidden_low, fc1, ((1,), (1,)))
        back_one = dot(grad_mixed, wq, ((1,), (1,)))
        both = back_one * ln1_gain + back_two * ln2_gain
        upstream = scatter_blocks(both.astype(BF).reshape(T, rows, width))
        own_hat, own_factor = norm_parts(own_f32)
        back = own_factor * (
            upstream
            - jnp.mean(upstream, axis=-1, keepdims=True)
            - own_hat * jnp.mean(upstream * own_hat, axis=-1, keepdims=True)
        )
        own_grad_f32 = own_grad.astype(F32)
        grad_tokens = (own_grad_f32 + back).astype(BF)

        dense_term = dot(attention_low, grads, ((0,), (0,))).astype(BF)
        qkv_term = dot(normed_one, grad_mixed, ((0,), (0,))).astype(BF)
        total = F * C
        part = width // total
        g_fc2 = reduce_rest(fc2_term.reshape(1, R, cols // R, width), ri, True)[0]
        g_fc1 = reduce_rest(fc1_term.reshape(T, R, part, cols), ri, False)
        g_fc1 = columns_back(g_fc1, t, fi, half)
        grad_w_fc1 = jnp.moveaxis(g_fc1, 0, 1).reshape(part, hidden_width)
        g_dense = reduce_rest(dense_term.reshape(1, R, head // R, width), ri, True)[0]
        g_qkv = reduce_rest(qkv_term.reshape(T, R, part, 3 * head), ri, True)
        g_qkv = columns_back(g_qkv, t, fi, half)
        grad_w_qkv = jnp.transpose(g_qkv.reshape(T, part, 3, head), (1, 2, 0, 3)).reshape(
            part, 3 * width
        )

        here = (jnp.arange(T, dtype=jnp.int32) == t).astype(F32)
        sum_hidden = jnp.sum(grad_hidden_low.astype(F32), axis=0)
        sum_mixed = jnp.sum(grad_mixed.astype(F32), axis=0).reshape(3, head)
        packed = jnp.concatenate(
            [
                jnp.sum(back_one * xhat, axis=0).reshape(total, part),
                jnp.sum(back_one, axis=0).reshape(total, part),
                jnp.sum(back_two * xhat, axis=0).reshape(total, part),
                jnp.sum(back_two, axis=0).reshape(total, part),
                jnp.sum(own_grad_f32, axis=0).reshape(total, part),
                (sum_mixed[:, None, :] * here[None, :, None]).reshape(total, 3 * part),
                (sum_hidden[None, :] * here[:, None]).reshape(total, cols // R),
            ],
            axis=1,
        )
        current = packed
        for k in reversed(range(fbits)):
            current = current.reshape((2, -1) + current.shape[1:])
            mine = (fi >> k) & 1
            current = pick(current, mine) + swap_f(pick(current, 1 - mine), 1 << k)
        for k in reversed(range(bits + 1)):
            current = current.reshape((2, -1) + current.shape[1:])
            mine = (ci >> k) & 1
            current = pick(current, mine) + swap_c(pick(current, 1 - mine), 1 << k)
        vector = current.reshape(-1)
        grad_b_out = vector[4 * part : 5 * part]
        return (
            output.reshape(tokens.shape),
            grad_tokens.reshape(tokens.shape),
            vector[:part],
            vector[part : 2 * part],
            vector[2 * part : 3 * part],
            vector[3 * part : 4 * part],
            grad_w_qkv,
            vector[5 * part : 8 * part],
            g_dense,
            grad_b_out,
            grad_w_fc1,
            vector[8 * part :],
            g_fc2,
            grad_b_out,
        )

    return shards


def solution(mesh):
    in_specs = (
        P("fsdp", "ctx", None),
        P(),
        P(),
        P(),
        P(),
        P(),
        P("fsdp", None),
        P(),
        P("fsdp", None),
        P(),
        P("fsdp", None),
        P(),
        P("fsdp", None),
        P(),
        P("fsdp", "ctx", None),
    )
    both = ("fsdp", "ctx")
    out_specs = (
        P("fsdp", "ctx", None),
        P("fsdp", "ctx", None),
        P(both),
        P(both),
        P(both),
        P(both),
        P(both, None),
        P(both),
        P(both, None),
        P(both),
        P(both, None),
        P(both),
        P(both, None),
        P(both),
    )
    shards = make_shards(mesh.shape["fsdp"], mesh.shape["ctx"])
    return jax.shard_map(shards, mesh=mesh, in_specs=in_specs, out_specs=out_specs, check_vma=False)
```

```python
import jax
import jax.numpy as jnp
from jax import lax
from jax.sharding import PartitionSpec as P


HEADS = 8
HEAD_DIM = 256
ROTARY = 64

epsilon = 1e-05
big_negative = -1e30
BF = jnp.bfloat16
F32 = jnp.float32


def angles_of(positions):
    inverse_rate = 10000.0 ** (-jnp.arange(0, ROTARY, 2, dtype=F32) / ROTARY)
    phase = positions.astype(F32)[:, None] * inverse_rate[None, :]
    phase = jnp.concatenate([phase, phase], axis=-1)
    return (jnp.cos(phase), jnp.sin(phase))


def rotate(values, cosine, sine):
    head_part = values[..., :ROTARY]
    middle = ROTARY // 2
    turned = jnp.concatenate([-head_part[..., middle:], head_part[..., :middle]], axis=-1)
    mixed = head_part * cosine + turned * sine
    return jnp.concatenate([mixed, values[..., ROTARY:]], axis=-1)


def rotate_back(values, cosine, sine):
    head_part = values[..., :ROTARY]
    middle = ROTARY // 2
    scaled = head_part * sine
    turned = jnp.concatenate([scaled[..., middle:], -scaled[..., :middle]], axis=-1)
    mixed = head_part * cosine + turned
    return jnp.concatenate([mixed, values[..., ROTARY:]], axis=-1)


def gelu_parts(values):
    below = 0.5 + 0.5 * lax.erf(values * (0.5**0.5))
    bell = jnp.exp(-0.5 * values * values) * ((2.0 * jnp.pi) ** -0.5)
    return values * below, below + values * bell


def positions_of(block_order, slices, local_len):
    block = local_len // 2
    rows = (slices[:, None] * local_len + jnp.arange(local_len, dtype=jnp.int32)[None, :]).reshape(-1)
    places = rows // block
    table = places[:, None] == jnp.arange(block_order.shape[0], dtype=jnp.int32)[None, :]
    chosen = jnp.sum(jnp.where(table, block_order[None, :], 0), axis=1)
    return chosen * block + rows % block


def dot(left, right, dims):
    return lax.dot_general(left, right, (dims, ((), ())), preferred_element_type=F32)


def pick(array, index, axis=0):
    return lax.dynamic_index_in_dim(array, index, axis, keepdims=False)


def make_shards(F, C):
    R = C // 2
    T = 2 * F
    bits = R.bit_length() - 1
    assert R == 1 << bits and F & (F - 1) == 0

    def swap_f(array, mask):
        return lax.ppermute(array, "fsdp", [(i, i ^ mask) for i in range(F)])

    def swap_c(array, mask):
        return lax.ppermute(array, "ctx", [(i, i ^ mask) for i in range(C)])

    def swap_fc(array, fmask, cmask):
        if cmask == 0:
            return swap_f(array, fmask)
        if fmask == 0:
            return swap_c(array, cmask)
        pairs = [
            (i * C + j, (i ^ fmask) * C + (j ^ cmask)) for i in range(F) for j in range(C)
        ]
        return lax.ppermute(array, ("fsdp", "ctx"), pairs)

    fbits = F.bit_length() - 1

    def bit_mirror(value):
        out = value * 0
        for k in range(fbits):
            out = out | (((value >> k) & 1) << (fbits - 1 - k))
        return out

    def gather_blocks(own):
        far = swap_c(own, R)
        pieces = [own, far]
        if fbits > 1:
            pieces = pieces + [swap_f(own, F // 2), swap_f(far, F // 2)]
        current = jnp.concatenate(pieces, axis=0)
        for k in reversed(range(max(fbits - 1, 1))):
            current = jnp.concatenate([current, swap_f(current, 1 << k)], axis=0)
        return current

    def scatter_blocks(array):
        current = array
        total = None
        for k in range(fbits):
            rest = current.shape[0] // 2
            got = swap_f(current[rest:], 1 << k)
            total = current[:rest].astype(F32) + got.astype(F32)
            current = total.astype(BF)
        got = swap_c(current[1:], R)
        return total[0] + got[0].astype(F32)

    def columns_of_rows(slice_of, rows, cols, fi, ri):
        part = rows // 2
        mine = (ri & 1) * part
        out = lax.dynamic_update_slice(
            jnp.zeros((F * rows, cols), BF), slice_of(fi, 0, rows), (fi * rows, 0)
        )
        got = swap_f(slice_of(fi ^ 1, 0, rows), 1)
        out = lax.dynamic_update_slice(out, got, ((fi ^ 1) * rows, 0))
        far = [swap_f(slice_of(fi ^ e, mine, part), e) for e in range(2, F)]
        for e, block in zip(range(2, F), far):
            out = lax.dynamic_update_slice(out, block, ((fi ^ e) * rows + mine, 0))
            block = swap_c(block, 1)
            out = lax.dynamic_update_slice(out, block, ((fi ^ e) * rows + part - mine, 0))
        return out

    def reduce_rest(array, ri, first_low):
        lead = array.shape[0]
        tail = array.shape[2:]
        order_bits = list(range(bits)) if first_low else list(reversed(range(bits)))
        current = array.reshape((lead,) + (2,) * bits + tail)
        live = list(reversed(range(bits)))
        for k in order_bits:
            axis = 1 + live.index(k)
            mine = (ri >> k) & 1
            sent = pick(current, 1 - mine, axis).astype(BF)
            kept = pick(current, mine, axis)
            got = swap_c(sent, 1 << k)
            current = kept.astype(F32) + got.astype(F32)
            live.remove(k)
        return current

    def columns_back(array, t):
        low = array.astype(BF)
        blocks = []
        for e in range(T):
            sent = pick(low, t ^ e)
            blocks.append(sent if e == 0 else swap_fc(sent, e >> 1, R * (e & 1)))
        return blocks

    def exchange_in(array, rows, ri):
        parts = []
        for s in range(R):
            start = bit_mirror(ri ^ s) * rows
            sent = lax.dynamic_slice(array, (start, 0), (rows, array.shape[1]))
            parts.append(sent if s == 0 else swap_c(sent, s))
        return jnp.concatenate(parts, axis=0)

    def exchange_out(array, rows, ri):
        out = jnp.zeros(array.shape, array.dtype)
        for s in range(R):
            sent = array[s * rows : (s + 1) * rows]
            got = sent if s == 0 else swap_c(sent, s)
            out = lax.dynamic_update_slice(out, got, (bit_mirror(ri ^ s) * rows, 0))
        return out

    def spread_attention(qkv, grad_heads, block_order, half, ri, local_len):
        scale = HEAD_DIM ** (-0.5)
        rows = 2 * local_len
        whole = exchange_in(qkv, rows, ri)
        grads = exchange_in(grad_heads, rows, ri)
        slices = jnp.stack(
            [(half ^ j) * R + (ri ^ s) for s in range(R) for j in range(2)]
        ).astype(jnp.int32)
        pos = positions_of(block_order, slices, local_len)
        query = whole[:, :HEAD_DIM]
        key = whole[:, HEAD_DIM : 2 * HEAD_DIM]
        value = whole[:, 2 * HEAD_DIM :]
        visible = pos[None, :] <= pos[:, None]
        scores = dot(query, key, ((1,), (1,))) * scale
        scores = jnp.where(visible, scores, big_negative)
        top = jnp.max(scores, axis=-1, keepdims=True)
        weights = jnp.where(visible, jnp.exp(scores - top), 0.0)
        probs = weights / jnp.sum(weights, axis=-1, keepdims=True)
        probs_low = probs.astype(BF)
        attention = dot(probs_low, value, ((1,), (0,)))
        attention_low = exchange_out(attention.astype(BF), rows, ri)
        delta = jnp.sum(grads.astype(F32) * attention, axis=-1, keepdims=True)
        grad_probs = dot(grads, value, ((1,), (1,)))
        grad_scores = (probs * (grad_probs - delta)).astype(BF)
        grad_query = dot(grad_scores, key, ((1,), (0,))) * scale
        grad_key = dot(grad_scores, query, ((0,), (0,))) * scale
        grad_value = dot(probs_low, grads, ((0,), (0,)))
        cosine, sine = angles_of(pos)
        results = jnp.concatenate(
            [
                rotate_back(grad_query, cosine, sine).astype(BF),
                rotate_back(grad_key, cosine, sine).astype(BF),
                grad_value.astype(BF),
            ],
            axis=1,
        )
        return attention_low, exchange_out(results, rows, ri)

    def gathered_attention(qkv, grad_heads, block_order, half, ri, local_len):
        scale = HEAD_DIM ** (-0.5)
        qkv = qkv.reshape(-1, 2 * local_len, 3, HEAD_DIM)
        grad_heads = grad_heads.reshape(-1, 2 * local_len, HEAD_DIM)
        query, pair = qkv[:, :, 0], qkv[:, :, 1:]
        pairs = pair[None]
        for k in range(bits):
            pairs = jnp.concatenate([pairs, swap_c(pairs, 1 << k)], axis=0)
        my_slices = jnp.stack([(half ^ j) * R + ri for j in range(2)]).astype(jnp.int32)
        all_slices = jnp.stack(
            [(half ^ j) * R + (ri ^ s) for s in range(R) for j in range(2)]
        ).astype(jnp.int32)
        pos = positions_of(block_order, my_slices, local_len)
        key_pos = positions_of(block_order, all_slices, local_len)
        key = jnp.moveaxis(pairs[:, :, :, 0], 0, 1).reshape(qkv.shape[0], -1, HEAD_DIM)
        value = jnp.moveaxis(pairs[:, :, :, 1], 0, 1).reshape(qkv.shape[0], -1, HEAD_DIM)
        visible = (key_pos[None, :] <= pos[:, None])[None]

        def product(spec, a, b):
            return jnp.einsum(spec, a, b, preferred_element_type=F32)

        scores = jnp.where(visible, product("sqd,skd->sqk", query, key) * scale, big_negative)
        top = jnp.max(scores, axis=-1, keepdims=True)
        weights = jnp.where(visible, jnp.exp(scores - top), 0.0)
        probs = weights / jnp.sum(weights, axis=-1, keepdims=True)
        probs_low = probs.astype(BF)
        attention = product("sqk,skd->sqd", probs_low, value)
        delta = jnp.sum(grad_heads.astype(F32) * attention, axis=-1, keepdims=True)
        grad_probs = product("sqd,skd->sqk", grad_heads, value)
        grad_scores = (probs * (grad_probs - delta)).astype(BF)
        grad_query = product("sqk,skd->sqd", grad_scores, key) * scale
        grad_key = product("sqk,sqd->skd", grad_scores, query) * scale
        grad_value = product("sqk,sqd->skd", probs_low, grad_heads)
        both = jnp.stack([grad_key, grad_value], axis=2)
        both = both.reshape((qkv.shape[0], R, qkv.shape[1], 2, HEAD_DIM))
        both = jnp.moveaxis(both, 1, 0)
        for k in reversed(range(bits)):
            rest = both.shape[0] // 2
            both = both[:rest] + swap_c(both[rest:], 1 << k)
        cosine, sine = angles_of(pos)
        grad_mixed = jnp.stack(
            [
                rotate_back(grad_query, cosine, sine),
                rotate_back(both[0, :, :, 0], cosine, sine),
                both[0, :, :, 1],
            ],
            axis=2,
        ).astype(BF)
        return attention.astype(BF).reshape(-1, HEAD_DIM), grad_mixed.reshape(-1, 3 * HEAD_DIM)

    def shards(
        tokens,
        block_order,
        ln1_gain,
        ln1_bias,
        ln2_gain,
        ln2_bias,
        w_qkv,
        b_qkv,
        w_dense,
        b_dense,
        w_fc1,
        b_fc1,
        w_fc2,
        b_fc2,
        cotangent,
    ):
        seqs, local_len, width = tokens.shape
        hidden_width = w_fc1.shape[1]
        rows = seqs * local_len
        head = HEADS // T * HEAD_DIM
        assert head == HEAD_DIM
        cols = hidden_width // T
        fi = lax.axis_index("fsdp")
        ci = lax.axis_index("ctx")
        half = ci // R
        ri = ci % R
        t = fi * 2 + half

        assert seqs == 1
        own = tokens.reshape(rows, width)
        own_grad = cotangent.reshape(rows, width)
        inputs = gather_blocks(own).astype(F32)

        def qkv_columns(place, top, size):
            start = (place * 2 + half) * head
            return jnp.concatenate(
                [
                    lax.dynamic_slice(w_qkv, (top, j * width + start), (size, head))
                    for j in range(3)
                ],
                axis=1,
            )

        def fc1_columns(place, top, size):
            start = (place * 2 + half) * cols
            return lax.dynamic_slice(w_fc1, (top, start), (size, cols))

        wq = columns_of_rows(qkv_columns, w_qkv.shape[0], 3 * head, fi, ri)
        grads = gather_blocks(own_grad)
        fc1 = columns_of_rows(fc1_columns, w_fc1.shape[0], cols, fi, ri)

        def norm_parts(values):
            center = values - jnp.mean(values, axis=-1, keepdims=True)
            spread = jnp.mean(center * center, axis=-1, keepdims=True)
            factor = lax.rsqrt(spread + epsilon)
            return center * factor, factor

        xhat, _ = norm_parts(inputs)
        normed_one = (xhat * ln1_gain + ln1_bias).astype(BF)
        normed_two = (xhat * ln2_gain + ln2_bias).astype(BF)

        fc2 = pick(w_fc2.reshape(2, cols, width), half)
        bias_one = pick(b_fc1.reshape(T, cols), t)
        hidden = dot(normed_two, fc1, ((1,), (0,))) + bias_one
        activated, slope = gelu_parts(hidden)
        activated_low = activated.astype(BF)
        grad_hidden = dot(grads, fc2, ((1,), (1,))) * slope
        grad_hidden_low = grad_hidden.astype(BF)
        sum_hidden = jnp.sum(grad_hidden_low.astype(F32), axis=0)
        fc2_term = dot(activated_low, grads, ((0,), (0,))).astype(BF)
        fc1_term = dot(normed_two, grad_hidden_low, ((0,), (0,))).astype(BF)

        dense = pick(w_dense.reshape(2, head, width), half)
        bias = pick(b_qkv.reshape(3, T, head), t, 1)
        my_slices = jnp.stack([(half ^ j) * R + ri for j in range(2)]).astype(jnp.int32)
        cosine, sine = angles_of(positions_of(block_order, my_slices, local_len))
        cosine = jnp.concatenate([cosine] * F, axis=0)
        sine = jnp.concatenate([sine] * F, axis=0)
        mixed = dot(normed_one, wq, ((1,), (0,))) + bias.reshape(1, 3 * head)
        qkv = jnp.concatenate(
            [
                rotate(mixed[:, :head], cosine, sine).astype(BF),
                rotate(mixed[:, head : 2 * head], cosine, sine).astype(BF),
                mixed[:, 2 * head :].astype(BF),
            ],
            axis=1,
        )
        grad_heads = dot(grads, dense, ((1,), (1,))).astype(BF)
        attend = spread_attention if F == R else gathered_attention
        attention_low, grad_mixed = attend(qkv, grad_heads, block_order, half, ri, local_len)

        partial = lax.optimization_barrier(dot(activated_low, fc2, ((1,), (0,))))
        partial = partial + dot(attention_low, dense, ((1,), (0,)))
        summed = scatter_blocks(partial.astype(BF).reshape(T, rows, width))
        own_f32 = own.astype(F32)
        output = (own_f32 + (summed + b_dense + b_fc2)).astype(BF)

        back_two = lax.optimization_barrier(dot(grad_hidden_low, fc1, ((1,), (1,))))
        back_one = dot(grad_mixed, wq, ((1,), (1,)))
        both = back_one * ln1_gain + back_two * ln2_gain
        norm_sums = [
            jnp.sum(back_one * xhat, axis=0),
            jnp.sum(back_one, axis=0),
            jnp.sum(back_two * xhat, axis=0),
            jnp.sum(back_two, axis=0),
        ]
        upstream = scatter_blocks(both.astype(BF).reshape(T, rows, width))
        own_hat, own_factor = norm_parts(own_f32)
        back = own_factor * (
            upstream
            - jnp.mean(upstream, axis=-1, keepdims=True)
            - own_hat * jnp.mean(upstream * own_hat, axis=-1, keepdims=True)
        )
        own_grad_f32 = own_grad.astype(F32)
        grad_tokens = (own_grad_f32 + back).astype(BF)

        dense_term = dot(attention_low, grads, ((0,), (0,))).astype(BF)
        qkv_term = dot(normed_one, grad_mixed, ((0,), (0,))).astype(BF)
        total = F * C
        part = width // total
        g_fc2 = reduce_rest(fc2_term.reshape(1, R, cols // R, width), ri, True)[0]
        g_fc1 = reduce_rest(fc1_term.reshape(T, R, part, cols), ri, False)
        grad_w_fc1 = jnp.zeros((part, hidden_width), F32)
        for e, block in enumerate(columns_back(g_fc1, t)):
            grad_w_fc1 = lax.dynamic_update_slice(grad_w_fc1, block.astype(F32), (0, (t ^ e) * cols))
        g_dense = reduce_rest(dense_term.reshape(1, R, head // R, width), ri, False)[0]
        qkv_term = qkv_term.reshape(2, F, R, part, 3 * head)
        g_qkv = jnp.concatenate(
            [reduce_rest(qkv_term[0], ri, True), reduce_rest(qkv_term[1], ri, False)],
            axis=0,
        )
        grad_w_qkv = jnp.zeros((part, 3 * width), F32)
        for e, block in enumerate(columns_back(g_qkv, t)):
            for j in range(3):
                piece = block[:, j * head : (j + 1) * head].astype(F32)
                grad_w_qkv = lax.dynamic_update_slice(
                    grad_w_qkv, piece, (0, j * width + (t ^ e) * head)
                )

        here = (jnp.arange(T, dtype=jnp.int32) == t).astype(F32)
        sum_mixed = jnp.sum(grad_mixed.astype(F32), axis=0).reshape(3, head)
        packed = jnp.concatenate(
            [
                *[term.reshape(total, part) for term in norm_sums],
                jnp.sum(own_grad_f32, axis=0).reshape(total, part),
                (sum_mixed[:, None, :] * here[None, :, None]).reshape(total, 3 * part),
                (sum_hidden[None, :] * here[:, None]).reshape(total, cols // R),
            ],
            axis=1,
        )
        current = packed
        for k in reversed(range(fbits)):
            current = current.reshape((2, -1) + current.shape[1:])
            mine = (fi >> k) & 1
            current = pick(current, mine) + swap_f(pick(current, 1 - mine), 1 << k)
        for k in reversed(range(bits + 1)):
            current = current.reshape((2, -1) + current.shape[1:])
            mine = (ci >> k) & 1
            current = pick(current, mine) + swap_c(pick(current, 1 - mine), 1 << k)
        vector = current.reshape(-1)
        grad_b_out = vector[4 * part : 5 * part]
        return (
            output.reshape(tokens.shape),
            grad_tokens.reshape(tokens.shape),
            vector[:part],
            vector[part : 2 * part],
            vector[2 * part : 3 * part],
            vector[3 * part : 4 * part],
            grad_w_qkv,
            vector[5 * part : 8 * part],
            g_dense,
            grad_b_out,
            grad_w_fc1,
            vector[8 * part :],
            g_fc2,
            grad_b_out,
        )

    return shards


def solution(mesh):
    in_specs = (
        P("fsdp", "ctx", None),
        P(),
        P(),
        P(),
        P(),
        P(),
        P("fsdp", None),
        P(),
        P("fsdp", None),
        P(),
        P("fsdp", None),
        P(),
        P("fsdp", None),
        P(),
        P("fsdp", "ctx", None),
    )
    both = ("fsdp", "ctx")
    out_specs = (
        P("fsdp", "ctx", None),
        P("fsdp", "ctx", None),
        P(both),
        P(both),
        P(both),
        P(both),
        P(both, None),
        P(both),
        P(both, None),
        P(both),
        P(both, None),
        P(both),
        P(both, None),
        P(both),
    )
    shards = make_shards(mesh.shape["fsdp"], mesh.shape["ctx"])
    return jax.shard_map(shards, mesh=mesh, in_specs=in_specs, out_specs=out_specs, check_vma=False)
```

```python
import jax
import jax.numpy as jnp
from jax import lax
from jax.sharding import PartitionSpec as P


HEADS = 8
HEAD_DIM = 256
ROTARY = 64

epsilon = 1e-05
big_negative = -1e30
BF = jnp.bfloat16
F32 = jnp.float32


def angles_of(positions):
    inverse_rate = 10000.0 ** (-jnp.arange(0, ROTARY, 2, dtype=F32) / ROTARY)
    phase = positions.astype(F32)[:, None] * inverse_rate[None, :]
    phase = jnp.concatenate([phase, phase], axis=-1)
    return (jnp.cos(phase), jnp.sin(phase))


def rotate(values, cosine, sine):
    head_part = values[..., :ROTARY]
    middle = ROTARY // 2
    turned = jnp.concatenate([-head_part[..., middle:], head_part[..., :middle]], axis=-1)
    mixed = head_part * cosine + turned * sine
    return jnp.concatenate([mixed, values[..., ROTARY:]], axis=-1)


def rotate_back(values, cosine, sine):
    head_part = values[..., :ROTARY]
    middle = ROTARY // 2
    scaled = head_part * sine
    turned = jnp.concatenate([scaled[..., middle:], -scaled[..., :middle]], axis=-1)
    mixed = head_part * cosine + turned
    return jnp.concatenate([mixed, values[..., ROTARY:]], axis=-1)


def gelu_parts(values):
    below = 0.5 + 0.5 * lax.erf(values * (0.5**0.5))
    bell = jnp.exp(-0.5 * values * values) * ((2.0 * jnp.pi) ** -0.5)
    return values * below, below + values * bell


def positions_of(block_order, slices, local_len):
    block = local_len // 2
    rows = (slices[:, None] * local_len + jnp.arange(local_len, dtype=jnp.int32)[None, :]).reshape(-1)
    places = rows // block
    table = places[:, None] == jnp.arange(block_order.shape[0], dtype=jnp.int32)[None, :]
    chosen = jnp.sum(jnp.where(table, block_order[None, :], 0), axis=1)
    return chosen * block + rows % block


def dot(left, right, dims):
    return lax.dot_general(left, right, (dims, ((), ())), preferred_element_type=F32)


def pick(array, index, axis=0):
    return lax.dynamic_index_in_dim(array, index, axis, keepdims=False)


def make_shards(F, C):
    R = C // 2
    T = 2 * F
    bits = R.bit_length() - 1
    assert R == 1 << bits and F & (F - 1) == 0

    def swap_f(array, mask):
        return lax.ppermute(array, "fsdp", [(i, i ^ mask) for i in range(F)])

    def swap_c(array, mask):
        return lax.ppermute(array, "ctx", [(i, i ^ mask) for i in range(C)])

    fbits = F.bit_length() - 1

    def bit_mirror(value):
        out = value * 0
        for k in range(fbits):
            out = out | (((value >> k) & 1) << (fbits - 1 - k))
        return out

    def gather_blocks(own):
        far = swap_c(own, R)
        pieces = [own, far]
        if fbits > 1:
            pieces = pieces + [swap_f(own, F // 2), swap_f(far, F // 2)]
        current = jnp.concatenate(pieces, axis=0)
        for k in reversed(range(max(fbits - 1, 1))):
            current = jnp.concatenate([current, swap_f(current, 1 << k)], axis=0)
        return current

    def scatter_blocks(kept, sent):
        for k in range(fbits):
            got = swap_f(sent, 1 << k)
            rest = got.shape[0] // 2
            sent = (kept[rest:].astype(F32) + got[rest:].astype(F32)).astype(BF)
            kept = kept[:rest].astype(F32) + got[:rest].astype(F32)
        got = swap_c(sent, R)
        return kept[0] + got[0].astype(F32)

    def columns_of_rows(slice_of, rows, cols, fi, ri):
        part = rows // 2
        bit = {e: (e & 1) % bits for e in range(2, F)}
        mine = {e: ((ri >> bit[e]) & 1) * part for e in range(2, F)}
        got = swap_f(slice_of(fi ^ 1, 0, rows), 1)
        out = lax.dynamic_update_slice(
            jnp.zeros((F * rows, cols), BF), slice_of(fi, 0, rows), (fi * rows, 0)
        )
        out = lax.dynamic_update_slice(out, got, ((fi ^ 1) * rows, 0))
        far = {e: swap_f(slice_of(fi ^ e, mine[e], part), e) for e in range(2, F)}
        for e, block in far.items():
            out = lax.dynamic_update_slice(out, block, ((fi ^ e) * rows + mine[e], 0))
        for e, block in far.items():
            block = swap_c(block, 1 << bit[e])
            out = lax.dynamic_update_slice(
                out, block, ((fi ^ e) * rows + part - mine[e], 0)
            )
        return out

    def reduce_rest(array, ri, first_low):
        lead = array.shape[0]
        tail = array.shape[2:]
        order_bits = list(range(bits)) if first_low else list(reversed(range(bits)))
        current = (array.reshape((lead,) + (2,) * bits + tail),)
        live = list(reversed(range(bits)))

        def total(place, axis):
            out = pick(current[0], place, axis).astype(F32)
            for more in current[1:]:
                out = out + pick(more, place, axis).astype(F32)
            return out

        for k in order_bits:
            axis = 1 + live.index(k)
            mine = (ri >> k) & 1
            sent = total(1 - mine, axis).astype(BF)
            kept = total(mine, axis) if len(current) > 1 else pick(current[0], mine, axis)
            current = (kept, swap_c(sent, 1 << k))
            live.remove(k)
        return current[0].astype(F32) + current[1].astype(F32)

    def columns_back(array, fi, half, near_first):
        held = {0: array.reshape((2,) * (fbits + 1) + array.shape[1:])}
        live = list(range(fbits, -1, -1))
        stages = [0] + list(range(fbits, 0, -1))
        for bit in stages[1:] + stages[:1] if near_first else stages:
            axis = live.index(bit)
            mine = half if bit == 0 else (fi >> (bit - 1)) & 1
            keys = sorted(held)
            sent = jnp.stack([pick(held[key], 1 - mine, axis) for key in keys])
            if bit == 0:
                got = swap_c(sent, R)
            else:
                got = swap_f(sent, 1 << (bit - 1))
            placed = {}
            for at, key in enumerate(keys):
                kept = pick(held[key], mine, axis)
                placed[key] = jnp.where(mine == 0, kept, got[at])
                placed[key | (1 << bit)] = jnp.where(mine == 0, got[at], kept)
            held = placed
            live.remove(bit)
        return [held[place] for place in range(T)]

    def exchange_in(array, rows, ri):
        parts = []
        for s in range(R):
            start = bit_mirror(ri ^ s) * rows
            sent = lax.dynamic_slice(array, (start, 0), (rows, array.shape[1]))
            parts.append(sent if s == 0 else swap_c(sent, s))
        return jnp.concatenate(parts, axis=0)

    def in_place_order(blocks, ri):
        for k in range(bits):
            odd = ((ri >> k) & 1) == 1
            blocks = [jnp.where(odd, blocks[p ^ (1 << k)], blocks[p]) for p in range(R)]
        return jnp.concatenate([blocks[bit_mirror(j)] for j in range(R)], axis=0)

    def exchange_out(array, rows, ri):
        parts = [array[s * rows : (s + 1) * rows] for s in range(R)]
        return in_place_order([swap_c(parts[s], s) if s else parts[0] for s in range(R)], ri)

    def spread_attention(qkv, grad_heads, block_order, half, ri, local_len):
        scale = HEAD_DIM ** (-0.5)
        rows = 2 * local_len
        whole = exchange_in(qkv, rows, ri)
        slices = jnp.stack(
            [(half ^ j) * R + (ri ^ s) for s in range(R) for j in range(2)]
        ).astype(jnp.int32)
        pos = positions_of(block_order, slices, local_len)
        query = whole[:, :HEAD_DIM]
        key = whole[:, HEAD_DIM : 2 * HEAD_DIM]
        value = whole[:, 2 * HEAD_DIM :]
        visible = pos[None, :] <= pos[:, None]
        scores = dot(query, key, ((1,), (1,))) * scale
        scores = jnp.where(visible, scores, big_negative)
        top = jnp.max(scores, axis=-1, keepdims=True)
        weights = jnp.where(visible, jnp.exp(scores - top), 0.0)
        probs = weights / jnp.sum(weights, axis=-1, keepdims=True)
        probs_low = probs.astype(BF)
        attention = dot(probs_low, value, ((1,), (0,)))
        attention, attention_low = lax.optimization_barrier((attention, attention.astype(BF)))
        got_low = []
        grads = []
        for s in range(R):
            start = bit_mirror(ri ^ s) * rows
            sent_low = attention_low[s * rows : (s + 1) * rows]
            sent_grad = lax.dynamic_slice(grad_heads, (start, 0), (rows, HEAD_DIM))
            if s:
                got = swap_c(jnp.concatenate([sent_low, sent_grad], axis=1), s)
                sent_low, sent_grad = got[:, :HEAD_DIM], got[:, HEAD_DIM:]
            grads.append(sent_grad)
            got_low.append(sent_low)
        grads = jnp.concatenate(grads, axis=0)
        delta = jnp.sum(grads.astype(F32) * attention, axis=-1, keepdims=True)
        grad_probs = dot(grads, value, ((1,), (1,)))
        grad_scores = (probs * (grad_probs - delta)).astype(BF)
        grad_query = dot(grad_scores, key, ((1,), (0,))) * scale
        grad_key = dot(grad_scores, query, ((0,), (0,))) * scale
        grad_value = dot(probs_low, grads, ((0,), (0,)))
        cosine, sine = angles_of(pos)
        results = jnp.concatenate(
            [
                rotate_back(grad_query, cosine, sine).astype(BF),
                rotate_back(grad_key, cosine, sine).astype(BF),
                grad_value.astype(BF),
            ],
            axis=1,
        )
        return in_place_order(got_low, ri), exchange_out(results, rows, ri)

    def gathered_attention(qkv, grad_heads, block_order, half, ri, local_len):
        scale = HEAD_DIM ** (-0.5)
        qkv = qkv.reshape(-1, 2 * local_len, 3, HEAD_DIM)
        grad_heads = grad_heads.reshape(-1, 2 * local_len, HEAD_DIM)
        query, pair = qkv[:, :, 0], qkv[:, :, 1:]
        pairs = pair[None]
        for k in range(bits):
            pairs = jnp.concatenate([pairs, swap_c(pairs, 1 << k)], axis=0)
        my_slices = jnp.stack([(half ^ j) * R + ri for j in range(2)]).astype(jnp.int32)
        all_slices = jnp.stack(
            [(half ^ j) * R + (ri ^ s) for s in range(R) for j in range(2)]
        ).astype(jnp.int32)
        pos = positions_of(block_order, my_slices, local_len)
        key_pos = positions_of(block_order, all_slices, local_len)
        key = jnp.moveaxis(pairs[:, :, :, 0], 0, 1).reshape(qkv.shape[0], -1, HEAD_DIM)
        value = jnp.moveaxis(pairs[:, :, :, 1], 0, 1).reshape(qkv.shape[0], -1, HEAD_DIM)
        visible = (key_pos[None, :] <= pos[:, None])[None]

        def product(spec, a, b):
            return jnp.einsum(spec, a, b, preferred_element_type=F32)

        scores = jnp.where(visible, product("sqd,skd->sqk", query, key) * scale, big_negative)
        top = jnp.max(scores, axis=-1, keepdims=True)
        weights = jnp.where(visible, jnp.exp(scores - top), 0.0)
        probs = weights / jnp.sum(weights, axis=-1, keepdims=True)
        probs_low = probs.astype(BF)
        attention = product("sqk,skd->sqd", probs_low, value)
        delta = jnp.sum(grad_heads.astype(F32) * attention, axis=-1, keepdims=True)
        grad_probs = product("sqd,skd->sqk", grad_heads, value)
        grad_scores = (probs * (grad_probs - delta)).astype(BF)
        grad_query = product("sqk,skd->sqd", grad_scores, key) * scale
        grad_key = product("sqk,sqd->skd", grad_scores, query) * scale
        grad_value = product("sqk,sqd->skd", probs_low, grad_heads)
        both = jnp.stack([grad_key, grad_value], axis=2)
        both = both.reshape((qkv.shape[0], R, qkv.shape[1], 2, HEAD_DIM))
        both = jnp.moveaxis(both, 1, 0)
        for k in reversed(range(bits)):
            rest = both.shape[0] // 2
            both = both[:rest] + swap_c(both[rest:], 1 << k)
        cosine, sine = angles_of(pos)
        grad_mixed = jnp.stack(
            [
                rotate_back(grad_query, cosine, sine),
                rotate_back(both[0, :, :, 0], cosine, sine),
                both[0, :, :, 1],
            ],
            axis=2,
        ).astype(BF)
        return attention.astype(BF).reshape(-1, HEAD_DIM), grad_mixed.reshape(-1, 3 * HEAD_DIM)

    def shards(
        tokens,
        block_order,
        ln1_gain,
        ln1_bias,
        ln2_gain,
        ln2_bias,
        w_qkv,
        b_qkv,
        w_dense,
        b_dense,
        w_fc1,
        b_fc1,
        w_fc2,
        b_fc2,
        cotangent,
    ):
        seqs, local_len, width = tokens.shape
        hidden_width = w_fc1.shape[1]
        rows = seqs * local_len
        count = T * rows
        head = HEADS // T * HEAD_DIM
        assert head == HEAD_DIM
        cols = hidden_width // T
        fi = lax.axis_index("fsdp")
        ci = lax.axis_index("ctx")
        half = ci // R
        ri = ci % R
        t = fi * 2 + half

        assert seqs == 1
        own = tokens.reshape(rows, width)
        own_grad = cotangent.reshape(rows, width)
        inputs = gather_blocks(own).astype(F32)

        def qkv_columns(place, top, size):
            start = (place * 2 + half) * head
            return jnp.concatenate(
                [
                    lax.dynamic_slice(w_qkv, (top, j * width + start), (size, head))
                    for j in range(3)
                ],
                axis=1,
            )

        def fc1_columns(place, top, size):
            start = (place * 2 + half) * cols
            return lax.dynamic_slice(w_fc1, (top, start), (size, cols))

        wq = columns_of_rows(qkv_columns, w_qkv.shape[0], 3 * head, fi, ri)
        grads = gather_blocks(own_grad)
        fc1 = columns_of_rows(fc1_columns, w_fc1.shape[0], cols, fi, ri)

        def norm_parts(values):
            center = values - jnp.mean(values, axis=-1, keepdims=True)
            spread = jnp.mean(center * center, axis=-1, keepdims=True)
            factor = lax.rsqrt(spread + epsilon)
            return center * factor, factor

        xhat, _ = norm_parts(inputs)
        normed_one = (xhat * ln1_gain + ln1_bias).astype(BF)
        normed_two = (xhat * ln2_gain + ln2_bias).astype(BF)

        fc2 = pick(w_fc2.reshape(2, cols, width), half)
        bias_one = pick(b_fc1.reshape(T, cols), t)
        hidden = dot(normed_two, fc1, ((1,), (0,))) + bias_one
        activated, slope = gelu_parts(hidden)
        activated_low, slope = lax.optimization_barrier((activated.astype(BF), slope.astype(BF)))
        grad_hidden = dot(grads, fc2, ((1,), (1,))) * slope.astype(F32)
        grad_hidden_low = grad_hidden.astype(BF)
        sum_hidden = jnp.sum(grad_hidden_low.astype(F32), axis=0)
        fc2_term = dot(activated_low, grads, ((0,), (0,))).astype(BF)
        fc1_term = dot(normed_two, grad_hidden_low, ((0,), (0,))).astype(BF)

        dense = pick(w_dense.reshape(2, head, width), half)
        bias = pick(b_qkv.reshape(3, T, head), t, 1)
        my_slices = jnp.stack([(half ^ j) * R + ri for j in range(2)]).astype(jnp.int32)
        cosine, sine = angles_of(positions_of(block_order, my_slices, local_len))
        cosine = jnp.concatenate([cosine] * F, axis=0)
        sine = jnp.concatenate([sine] * F, axis=0)
        mixed = dot(normed_one, wq, ((1,), (0,))) + bias.reshape(1, 3 * head)
        qkv = jnp.concatenate(
            [
                rotate(mixed[:, :head], cosine, sine).astype(BF),
                rotate(mixed[:, head : 2 * head], cosine, sine).astype(BF),
                mixed[:, 2 * head :].astype(BF),
            ],
            axis=1,
        )
        grad_heads = dot(grads, dense, ((1,), (1,))).astype(BF)
        attend = spread_attention if F == R else gathered_attention
        attention_low, grad_mixed = attend(qkv, grad_heads, block_order, half, ri, local_len)

        fed = lax.optimization_barrier(dot(activated_low, fc2, ((1,), (0,))).astype(BF))
        lower = count // 2
        halves = []
        for at in (lower, 0):
            term = dot(attention_low[at : at + lower], dense, ((1,), (0,)))
            term = (fed[at : at + lower].astype(F32) + term).astype(BF)
            halves.append(term.reshape(T // 2, rows, width))
        summed = scatter_blocks(halves[1], halves[0])
        own_f32 = own.astype(F32)
        output = (own_f32 + (summed + b_dense + b_fc2)).astype(BF)

        back_two = dot(grad_hidden_low, fc1, ((1,), (1,)))
        norm_two = [jnp.sum(back_two * xhat, axis=0), jnp.sum(back_two, axis=0)]
        back_two = lax.optimization_barrier((back_two * ln2_gain).astype(BF))
        norm_one = [0.0, 0.0]
        halves = []
        for at in (lower, 0):
            back_one = dot(grad_mixed[at : at + lower], wq, ((1,), (1,)))
            term = back_one * ln1_gain + back_two[at : at + lower].astype(F32)
            norm_one[0] = norm_one[0] + jnp.sum(back_one * xhat[at : at + lower], axis=0)
            norm_one[1] = norm_one[1] + jnp.sum(back_one, axis=0)
            halves.append(term.astype(BF).reshape(T // 2, rows, width))
        upstream = scatter_blocks(halves[1], halves[0])
        norm_sums = norm_one + norm_two
        own_hat, own_factor = norm_parts(own_f32)
        own_grad_f32 = own_grad.astype(F32)
        back = own_factor * (
            upstream
            - jnp.mean(upstream, axis=-1, keepdims=True)
            - own_hat * jnp.mean(upstream * own_hat, axis=-1, keepdims=True)
        )
        grad_tokens = (own_grad_f32 + back).astype(BF)

        dense_term = dot(attention_low, grads, ((0,), (0,))).astype(BF)
        qkv_term = dot(normed_one, grad_mixed, ((0,), (0,))).astype(BF)
        total = F * C
        part = width // total
        fc2_term = fc2_term.reshape(1, R, 2, cols // R // 2, width)
        g_fc2 = jnp.concatenate(
            [
                reduce_rest(fc2_term[:, :, 0], ri, True)[0],
                reduce_rest(fc2_term[:, :, 1], ri, True)[0],
            ],
            axis=0,
        )
        fc1_term = fc1_term.reshape(2, F, R, part, cols)
        g_fc1 = jnp.concatenate(
            [
                reduce_rest(fc1_term[0], ri, True).astype(BF),
                reduce_rest(fc1_term[1], ri, False).astype(BF),
            ],
            axis=0,
        )
        blocks = columns_back(g_fc1, fi, half, False)
        grad_w_fc1 = jnp.concatenate([block.astype(F32) for block in blocks], axis=1)
        g_dense = reduce_rest(dense_term.reshape(1, R, head // R, width), ri, True)[0]
        qkv_term = qkv_term.reshape(2, F, R, part, 3 * head)
        g_qkv = jnp.concatenate(
            [
                reduce_rest(qkv_term[0], ri, True).astype(BF),
                reduce_rest(qkv_term[1], ri, False).astype(BF),
            ],
            axis=0,
        )
        blocks = columns_back(g_qkv, fi, half, False)
        grad_w_qkv = jnp.concatenate(
            [block[:, j * head : (j + 1) * head].astype(F32) for j in range(3) for block in blocks],
            axis=1,
        )

        sum_mixed = jnp.sum(grad_mixed.astype(F32), axis=0).reshape(3, head)
        all_mixed = lax.dynamic_update_slice(jnp.zeros((3, width), F32), sum_mixed, (0, t * head))
        all_hidden = lax.dynamic_update_slice(
            jnp.zeros((hidden_width,), F32), sum_hidden, (t * cols,)
        ).reshape(hidden_width // width, width)
        lines = norm_sums + [jnp.sum(own_grad_f32, axis=0)]
        current = jnp.concatenate(
            [line[None, :] for line in lines] + [all_mixed, all_hidden], axis=0
        )
        for k in reversed(range(fbits)):
            got = swap_f(current, 1 << k)
            current = current + got
        for k in list(reversed(range(bits))) + [bits]:
            got = swap_c(current, 1 << k)
            current = current + got
        place = fi * C + ci
        sums = [lax.dynamic_slice(current[i], (place * part,), (part,)) for i in range(5)]
        for top, end in ((5, 8), (8, 8 + hidden_width // width)):
            wide = current[top:end].reshape(-1)
            each = (end - top) * part
            sums.append(lax.dynamic_slice(wide, (place * each,), (each,)))
        grad_b_out = sums[4]
        return (
            output.reshape(tokens.shape),
            grad_tokens.reshape(tokens.shape),
            *sums[:4],
            grad_w_qkv,
            sums[5],
            g_dense,
            grad_b_out,
            grad_w_fc1,
            sums[6],
            g_fc2,
            grad_b_out,
        )

    return shards


def solution(mesh):
    in_specs = (
        P("fsdp", "ctx", None),
        P(),
        P(),
        P(),
        P(),
        P(),
        P("fsdp", None),
        P(),
        P("fsdp", None),
        P(),
        P("fsdp", None),
        P(),
        P("fsdp", None),
        P(),
        P("fsdp", "ctx", None),
    )
    both = ("fsdp", "ctx")
    out_specs = (
        P("fsdp", "ctx", None),
        P("fsdp", "ctx", None),
        P(both),
        P(both),
        P(both),
        P(both),
        P(both, None),
        P(both),
        P(both, None),
        P(both),
        P(both, None),
        P(both),
        P(both, None),
        P(both),
    )
    shards = make_shards(mesh.shape["fsdp"], mesh.shape["ctx"])
    return jax.shard_map(shards, mesh=mesh, in_specs=in_specs, out_specs=out_specs, check_vma=False)
```

```python
import jax
import jax.numpy as jnp
from jax import lax
from jax.sharding import PartitionSpec as P


HEADS = 8
HEAD_DIM = 256
ROTARY = 64

epsilon = 1e-05
big_negative = -1e30
BF = jnp.bfloat16
F32 = jnp.float32


def angles_of(positions):
    inverse_rate = 10000.0 ** (-jnp.arange(0, ROTARY, 2, dtype=F32) / ROTARY)
    phase = positions.astype(F32)[:, None] * inverse_rate[None, :]
    phase = jnp.concatenate([phase, phase], axis=-1)
    return (jnp.cos(phase), jnp.sin(phase))


def rotate(values, cosine, sine):
    head_part = values[..., :ROTARY]
    middle = ROTARY // 2
    turned = jnp.concatenate([-head_part[..., middle:], head_part[..., :middle]], axis=-1)
    mixed = head_part * cosine + turned * sine
    return jnp.concatenate([mixed, values[..., ROTARY:]], axis=-1)


def rotate_back(values, cosine, sine):
    head_part = values[..., :ROTARY]
    middle = ROTARY // 2
    scaled = head_part * sine
    turned = jnp.concatenate([scaled[..., middle:], -scaled[..., :middle]], axis=-1)
    mixed = head_part * cosine + turned
    return jnp.concatenate([mixed, values[..., ROTARY:]], axis=-1)


def gelu_parts(values):
    below = 0.5 + 0.5 * lax.erf(values * (0.5**0.5))
    bell = jnp.exp(-0.5 * values * values) * ((2.0 * jnp.pi) ** -0.5)
    return values * below, below + values * bell


def positions_of(block_order, slices, local_len):
    block = local_len // 2
    rows = (slices[:, None] * local_len + jnp.arange(local_len, dtype=jnp.int32)[None, :]).reshape(-1)
    places = rows // block
    table = places[:, None] == jnp.arange(block_order.shape[0], dtype=jnp.int32)[None, :]
    chosen = jnp.sum(jnp.where(table, block_order[None, :], 0), axis=1)
    return chosen * block + rows % block


def dot(left, right, dims):
    return lax.dot_general(left, right, (dims, ((), ())), preferred_element_type=F32)


def pick(array, index, axis=0):
    return lax.dynamic_index_in_dim(array, index, axis, keepdims=False)


def make_shards(F, C):
    R = C // 2
    T = 2 * F
    bits = R.bit_length() - 1
    assert R == 1 << bits and F & (F - 1) == 0

    def swap_f(array, mask):
        return lax.ppermute(array, "fsdp", [(i, i ^ mask) for i in range(F)])

    def swap_c(array, mask):
        return lax.ppermute(array, "ctx", [(i, i ^ mask) for i in range(C)])

    fbits = F.bit_length() - 1

    def bit_mirror(value):
        out = value * 0
        for k in range(fbits):
            out = out | (((value >> k) & 1) << (fbits - 1 - k))
        return out

    def gather_blocks(own):
        far = swap_c(own, R)
        pieces = [own, far]
        if fbits > 1:
            pieces = pieces + [swap_f(own, F // 2), swap_f(far, F // 2)]
        current = jnp.concatenate(pieces, axis=0)
        for k in reversed(range(max(fbits - 1, 1))):
            current = jnp.concatenate([current, swap_f(current, 1 << k)], axis=0)
        return current

    def scatter_blocks(kept, sent):
        for k in range(fbits):
            got = swap_f(sent, 1 << k)
            rest = got.shape[0] // 2
            sent = (kept[rest:].astype(F32) + got[rest:].astype(F32)).astype(BF)
            kept = kept[:rest].astype(F32) + got[:rest].astype(F32)
        got = swap_c(sent, R)
        return kept[0] + got[0].astype(F32)

    def columns_of_rows(slice_of, rows, cols, fi, ri):
        part = rows // 2
        bit = {e: (e & 1) % bits for e in range(2, F)}
        mine = {e: ((ri >> bit[e]) & 1) * part for e in range(2, F)}
        got = swap_f(slice_of(fi ^ 1, 0, rows), 1)
        out = lax.dynamic_update_slice(
            jnp.zeros((F * rows, cols), BF), slice_of(fi, 0, rows), (fi * rows, 0)
        )
        out = lax.dynamic_update_slice(out, got, ((fi ^ 1) * rows, 0))
        far = {e: swap_f(slice_of(fi ^ e, mine[e], part), e) for e in range(2, F)}
        for e, block in far.items():
            out = lax.dynamic_update_slice(out, block, ((fi ^ e) * rows + mine[e], 0))
        for e, block in far.items():
            block = swap_c(block, 1 << bit[e])
            out = lax.dynamic_update_slice(
                out, block, ((fi ^ e) * rows + part - mine[e], 0)
            )
        return out

    def reduce_rest(array, ri, first_low):
        lead = array.shape[0]
        tail = array.shape[2:]
        order_bits = list(range(bits)) if first_low else list(reversed(range(bits)))
        current = (array.reshape((lead,) + (2,) * bits + tail),)
        live = list(reversed(range(bits)))

        def total(place, axis):
            out = pick(current[0], place, axis).astype(F32)
            for more in current[1:]:
                out = out + pick(more, place, axis).astype(F32)
            return out

        for k in order_bits:
            axis = 1 + live.index(k)
            mine = (ri >> k) & 1
            sent = total(1 - mine, axis).astype(BF)
            kept = total(mine, axis) if len(current) > 1 else pick(current[0], mine, axis)
            current = (kept, swap_c(sent, 1 << k))
            live.remove(k)
        return current[0].astype(F32) + current[1].astype(F32)

    def columns_back(array, fi, half, near_first):
        held = {0: array.reshape((2,) * (fbits + 1) + array.shape[1:])}
        live = list(range(fbits, -1, -1))
        stages = [0] + list(range(fbits, 0, -1))
        for bit in stages[1:] + stages[:1] if near_first else stages:
            axis = live.index(bit)
            mine = half if bit == 0 else (fi >> (bit - 1)) & 1
            keys = sorted(held)
            sent = jnp.stack([pick(held[key], 1 - mine, axis) for key in keys])
            if bit == 0:
                got = swap_c(sent, R)
            else:
                got = swap_f(sent, 1 << (bit - 1))
            placed = {}
            for at, key in enumerate(keys):
                kept = pick(held[key], mine, axis)
                placed[key] = jnp.where(mine == 0, kept, got[at])
                placed[key | (1 << bit)] = jnp.where(mine == 0, got[at], kept)
            held = placed
            live.remove(bit)
        return [held[place] for place in range(T)]

    def exchange_in(array, rows, ri):
        parts = []
        for s in range(R):
            start = bit_mirror(ri ^ s) * rows
            sent = lax.dynamic_slice(array, (start, 0), (rows, array.shape[1]))
            parts.append(sent if s == 0 else swap_c(sent, s))
        return jnp.concatenate(parts, axis=0)

    def in_place_order(blocks, ri):
        for k in range(bits):
            odd = ((ri >> k) & 1) == 1
            blocks = [jnp.where(odd, blocks[p ^ (1 << k)], blocks[p]) for p in range(R)]
        return jnp.concatenate([blocks[bit_mirror(j)] for j in range(R)], axis=0)

    def exchange_out(array, rows, ri):
        parts = [array[s * rows : (s + 1) * rows] for s in range(R)]
        return in_place_order([swap_c(parts[s], s) if s else parts[0] for s in range(R)], ri)

    def spread_attention(qkv, grad_heads, block_order, half, ri, local_len):
        scale = HEAD_DIM ** (-0.5)
        rows = 2 * local_len
        whole = exchange_in(qkv, rows, ri)
        slices = jnp.stack(
            [(half ^ j) * R + (ri ^ s) for s in range(R) for j in range(2)]
        ).astype(jnp.int32)
        pos = positions_of(block_order, slices, local_len)
        query = whole[:, :HEAD_DIM]
        key = whole[:, HEAD_DIM : 2 * HEAD_DIM]
        value = whole[:, 2 * HEAD_DIM :]
        visible = pos[None, :] <= pos[:, None]
        scores = dot(query, key, ((1,), (1,))) * scale
        scores = jnp.where(visible, scores, big_negative)
        top = jnp.max(scores, axis=-1, keepdims=True)
        weights = jnp.where(visible, jnp.exp(scores - top), 0.0)
        probs = weights / jnp.sum(weights, axis=-1, keepdims=True)
        probs_low = probs.astype(BF)
        attention = dot(probs_low, value, ((1,), (0,)))
        attention, attention_low = lax.optimization_barrier((attention, attention.astype(BF)))
        got_low = []
        grads = []
        for s in range(R):
            start = bit_mirror(ri ^ s) * rows
            sent_low = attention_low[s * rows : (s + 1) * rows]
            sent_grad = lax.dynamic_slice(grad_heads, (start, 0), (rows, HEAD_DIM))
            if s:
                got = swap_c(jnp.concatenate([sent_low, sent_grad], axis=1), s)
                sent_low, sent_grad = got[:, :HEAD_DIM], got[:, HEAD_DIM:]
            grads.append(sent_grad)
            got_low.append(sent_low)
        grads = jnp.concatenate(grads, axis=0)
        delta = jnp.sum(grads.astype(F32) * attention, axis=-1, keepdims=True)
        grad_probs = dot(grads, value, ((1,), (1,)))
        grad_scores = (probs * (grad_probs - delta)).astype(BF)
        grad_query = dot(grad_scores, key, ((1,), (0,))) * scale
        grad_key = dot(grad_scores, query, ((0,), (0,))) * scale
        grad_value = dot(probs_low, grads, ((0,), (0,)))
        cosine, sine = angles_of(pos)
        results = jnp.concatenate(
            [
                rotate_back(grad_query, cosine, sine).astype(BF),
                rotate_back(grad_key, cosine, sine).astype(BF),
                grad_value.astype(BF),
            ],
            axis=1,
        )
        return in_place_order(got_low, ri), exchange_out(results, rows, ri)

    def gathered_attention(qkv, grad_heads, block_order, half, ri, local_len):
        scale = HEAD_DIM ** (-0.5)
        qkv = qkv.reshape(-1, 2 * local_len, 3, HEAD_DIM)
        grad_heads = grad_heads.reshape(-1, 2 * local_len, HEAD_DIM)
        query, pair = qkv[:, :, 0], qkv[:, :, 1:]
        pairs = pair[None]
        for k in range(bits):
            pairs = jnp.concatenate([pairs, swap_c(pairs, 1 << k)], axis=0)
        my_slices = jnp.stack([(half ^ j) * R + ri for j in range(2)]).astype(jnp.int32)
        all_slices = jnp.stack(
            [(half ^ j) * R + (ri ^ s) for s in range(R) for j in range(2)]
        ).astype(jnp.int32)
        pos = positions_of(block_order, my_slices, local_len)
        key_pos = positions_of(block_order, all_slices, local_len)
        key = jnp.moveaxis(pairs[:, :, :, 0], 0, 1).reshape(qkv.shape[0], -1, HEAD_DIM)
        value = jnp.moveaxis(pairs[:, :, :, 1], 0, 1).reshape(qkv.shape[0], -1, HEAD_DIM)
        visible = (key_pos[None, :] <= pos[:, None])[None]

        def product(spec, a, b):
            return jnp.einsum(spec, a, b, preferred_element_type=F32)

        scores = jnp.where(visible, product("sqd,skd->sqk", query, key) * scale, big_negative)
        top = jnp.max(scores, axis=-1, keepdims=True)
        weights = jnp.where(visible, jnp.exp(scores - top), 0.0)
        probs = weights / jnp.sum(weights, axis=-1, keepdims=True)
        probs_low = probs.astype(BF)
        attention = product("sqk,skd->sqd", probs_low, value)
        delta = jnp.sum(grad_heads.astype(F32) * attention, axis=-1, keepdims=True)
        grad_probs = product("sqd,skd->sqk", grad_heads, value)
        grad_scores = (probs * (grad_probs - delta)).astype(BF)
        grad_query = product("sqk,skd->sqd", grad_scores, key) * scale
        grad_key = product("sqk,sqd->skd", grad_scores, query) * scale
        grad_value = product("sqk,sqd->skd", probs_low, grad_heads)
        both = jnp.stack([grad_key, grad_value], axis=2)
        both = both.reshape((qkv.shape[0], R, qkv.shape[1], 2, HEAD_DIM))
        both = jnp.moveaxis(both, 1, 0)
        for k in reversed(range(bits)):
            rest = both.shape[0] // 2
            both = both[:rest] + swap_c(both[rest:], 1 << k)
        cosine, sine = angles_of(pos)
        grad_mixed = jnp.stack(
            [
                rotate_back(grad_query, cosine, sine),
                rotate_back(both[0, :, :, 0], cosine, sine),
                both[0, :, :, 1],
            ],
            axis=2,
        ).astype(BF)
        return attention.astype(BF).reshape(-1, HEAD_DIM), grad_mixed.reshape(-1, 3 * HEAD_DIM)

    def shards(
        tokens,
        block_order,
        ln1_gain,
        ln1_bias,
        ln2_gain,
        ln2_bias,
        w_qkv,
        b_qkv,
        w_dense,
        b_dense,
        w_fc1,
        b_fc1,
        w_fc2,
        b_fc2,
        cotangent,
    ):
        seqs, local_len, width = tokens.shape
        hidden_width = w_fc1.shape[1]
        rows = seqs * local_len
        count = T * rows
        head = HEADS // T * HEAD_DIM
        assert head == HEAD_DIM
        cols = hidden_width // T
        fi = lax.axis_index("fsdp")
        ci = lax.axis_index("ctx")
        half = ci // R
        ri = ci % R
        t = fi * 2 + half

        assert seqs == 1
        own = tokens.reshape(rows, width)
        own_grad = cotangent.reshape(rows, width)
        inputs = gather_blocks(own).astype(F32)

        def qkv_columns(place, top, size):
            start = (place * 2 + half) * head
            return jnp.concatenate(
                [
                    lax.dynamic_slice(w_qkv, (top, j * width + start), (size, head))
                    for j in range(3)
                ],
                axis=1,
            )

        def fc1_columns(place, top, size):
            start = (place * 2 + half) * cols
            return lax.dynamic_slice(w_fc1, (top, start), (size, cols))

        wq = columns_of_rows(qkv_columns, w_qkv.shape[0], 3 * head, fi, ri)
        grads = gather_blocks(own_grad)
        fc1 = columns_of_rows(fc1_columns, w_fc1.shape[0], cols, fi, ri)

        def norm_parts(values):
            center = values - jnp.mean(values, axis=-1, keepdims=True)
            spread = jnp.mean(center * center, axis=-1, keepdims=True)
            factor = lax.rsqrt(spread + epsilon)
            return center * factor, factor

        xhat, _ = norm_parts(inputs)
        normed_one = (xhat * ln1_gain + ln1_bias).astype(BF)
        normed_two = (xhat * ln2_gain + ln2_bias).astype(BF)

        fc2 = pick(w_fc2.reshape(2, cols, width), half)
        bias_one = pick(b_fc1.reshape(T, cols), t)
        hidden = dot(normed_two, fc1, ((1,), (0,))) + bias_one
        activated, slope = gelu_parts(hidden)
        activated_low, slope = lax.optimization_barrier((activated.astype(BF), slope.astype(BF)))
        grad_hidden = dot(grads, fc2, ((1,), (1,))) * slope.astype(F32)
        grad_hidden_low = grad_hidden.astype(BF)
        sum_hidden = jnp.sum(grad_hidden_low.astype(F32), axis=0)
        fc2_term = dot(activated_low, grads, ((0,), (0,))).astype(BF)
        fc1_term = dot(normed_two, grad_hidden_low, ((0,), (0,))).astype(BF)

        dense = pick(w_dense.reshape(2, head, width), half)
        bias = pick(b_qkv.reshape(3, T, head), t, 1)
        my_slices = jnp.stack([(half ^ j) * R + ri for j in range(2)]).astype(jnp.int32)
        cosine, sine = angles_of(positions_of(block_order, my_slices, local_len))
        cosine = jnp.concatenate([cosine] * F, axis=0)
        sine = jnp.concatenate([sine] * F, axis=0)
        mixed = dot(normed_one, wq, ((1,), (0,))) + bias.reshape(1, 3 * head)
        qkv = jnp.concatenate(
            [
                rotate(mixed[:, :head], cosine, sine).astype(BF),
                rotate(mixed[:, head : 2 * head], cosine, sine).astype(BF),
                mixed[:, 2 * head :].astype(BF),
            ],
            axis=1,
        )
        grad_heads = dot(grads, dense, ((1,), (1,))).astype(BF)
        attend = spread_attention if F == R else gathered_attention
        attention_low, grad_mixed = attend(qkv, grad_heads, block_order, half, ri, local_len)

        fed = lax.optimization_barrier(dot(activated_low, fc2, ((1,), (0,))).astype(BF))
        lower = count // 2
        halves = []
        for at in (lower, 0):
            term = dot(attention_low[at : at + lower], dense, ((1,), (0,)))
            term = (fed[at : at + lower].astype(F32) + term).astype(BF)
            halves.append(term.reshape(T // 2, rows, width))
        summed = scatter_blocks(halves[1], halves[0])
        own_f32 = own.astype(F32)
        output = (own_f32 + (summed + b_dense + b_fc2)).astype(BF)

        back_two = dot(grad_hidden_low, fc1, ((1,), (1,)))
        norm_two = [jnp.sum(back_two * xhat, axis=0), jnp.sum(back_two, axis=0)]
        back_two = lax.optimization_barrier((back_two * ln2_gain).astype(BF))
        norm_one = [0.0, 0.0]
        halves = []
        for at in (lower, 0):
            back_one = dot(grad_mixed[at : at + lower], wq, ((1,), (1,)))
            term = back_one * ln1_gain + back_two[at : at + lower].astype(F32)
            norm_one[0] = norm_one[0] + jnp.sum(back_one * xhat[at : at + lower], axis=0)
            norm_one[1] = norm_one[1] + jnp.sum(back_one, axis=0)
            halves.append(term.astype(BF).reshape(T // 2, rows, width))
        upstream = scatter_blocks(halves[1], halves[0])
        norm_sums = norm_one + norm_two
        own_hat, own_factor = norm_parts(own_f32)
        own_grad_f32 = own_grad.astype(F32)
        back = own_factor * (
            upstream
            - jnp.mean(upstream, axis=-1, keepdims=True)
            - own_hat * jnp.mean(upstream * own_hat, axis=-1, keepdims=True)
        )
        grad_tokens = (own_grad_f32 + back).astype(BF)

        dense_term = dot(attention_low, grads, ((0,), (0,))).astype(BF)
        qkv_term = dot(normed_one, grad_mixed, ((0,), (0,))).astype(BF)
        total = F * C
        part = width // total
        fc2_term = fc2_term.reshape(1, R, 2, cols // R // 2, width)
        upper = reduce_rest(fc2_term[:, :, 0], ri, True)
        under = reduce_rest(fc2_term[:, :, 1], ri, True)
        upper = upper.reshape(upper.shape[1:])
        g_fc2 = jnp.concatenate([upper, under.reshape(under.shape[1:])], axis=0)
        fc1_term = fc1_term.reshape(2, F, R, part, cols)
        g_fc1 = jnp.concatenate(
            [
                reduce_rest(fc1_term[0], ri, True).astype(BF),
                reduce_rest(fc1_term[1], ri, False).astype(BF),
            ],
            axis=0,
        )
        blocks = columns_back(g_fc1, fi, half, False)
        grad_w_fc1 = jnp.concatenate([block.astype(F32) for block in blocks], axis=1)
        g_dense = reduce_rest(dense_term.reshape(1, R, head // R, width), ri, True)
        g_dense = g_dense.reshape(g_dense.shape[1:])
        qkv_term = qkv_term.reshape(2, F, R, part, 3 * head)
        g_qkv = jnp.concatenate(
            [
                reduce_rest(qkv_term[0], ri, True).astype(BF),
                reduce_rest(qkv_term[1], ri, False).astype(BF),
            ],
            axis=0,
        )
        blocks = columns_back(g_qkv, fi, half, True)
        grad_w_qkv = jnp.concatenate(
            [block[:, j * head : (j + 1) * head].astype(F32) for j in range(3) for block in blocks],
            axis=1,
        )

        sum_mixed = jnp.sum(grad_mixed.astype(F32), axis=0).reshape(3, head)
        all_mixed = lax.dynamic_update_slice(jnp.zeros((3, width), F32), sum_mixed, (0, t * head))
        all_hidden = lax.dynamic_update_slice(
            jnp.zeros((hidden_width,), F32), sum_hidden, (t * cols,)
        ).reshape(hidden_width // width, width)
        lines = norm_sums + [jnp.sum(own_grad_f32, axis=0)]
        current = jnp.concatenate(
            [line[None, :] for line in lines] + [all_mixed, all_hidden], axis=0
        )
        for k in reversed(range(fbits)):
            got = swap_f(current, 1 << k)
            current = current + got
        for k in list(reversed(range(bits))) + [bits]:
            got = swap_c(current, 1 << k)
            current = current + got
        place = fi * C + ci
        sums = [lax.dynamic_slice(current[i], (place * part,), (part,)) for i in range(5)]
        for top, end in ((5, 8), (8, 8 + hidden_width // width)):
            wide = current[top:end].reshape(-1)
            each = (end - top) * part
            sums.append(lax.dynamic_slice(wide, (place * each,), (each,)))
        grad_b_out = sums[4]
        return (
            output.reshape(tokens.shape),
            grad_tokens.reshape(tokens.shape),
            *sums[:4],
            grad_w_qkv,
            sums[5],
            g_dense,
            grad_b_out,
            grad_w_fc1,
            sums[6],
            g_fc2,
            grad_b_out,
        )

    return shards


def solution(mesh):
    in_specs = (
        P("fsdp", "ctx", None),
        P(),
        P(),
        P(),
        P(),
        P(),
        P("fsdp", None),
        P(),
        P("fsdp", None),
        P(),
        P("fsdp", None),
        P(),
        P("fsdp", None),
        P(),
        P("fsdp", "ctx", None),
    )
    both = ("fsdp", "ctx")
    out_specs = (
        P("fsdp", "ctx", None),
        P("fsdp", "ctx", None),
        P(both),
        P(both),
        P(both),
        P(both),
        P(both, None),
        P(both),
        P(both, None),
        P(both),
        P(both, None),
        P(both),
        P(both, None),
        P(both),
    )
    shards = make_shards(mesh.shape["fsdp"], mesh.shape["ctx"])
    return jax.shard_map(shards, mesh=mesh, in_specs=in_specs, out_specs=out_specs, check_vma=False)
```
